1024 devices in a mesh: ctx: 16 (over y, core), dp: 16 (over z), pipe: 4 (over x).
Axes of the slice: x: 4, y: 8, z: 16, core: 2. Of those that a mesh axis runs over, the one named last changes fastest.
Arguments:
- queries: bfloat16 [1, 16384, 8192], P(None, 'ctx', ('dp', 'pipe')), may hold values from -2 to 2
- key_tokens: bfloat16 [1, 16384, 8192], P(None, 'ctx', ('dp', 'pipe')), may hold values from -2 to 2
- values: bfloat16 [1, 16384, 8192], P(None, 'ctx', ('dp', 'pipe')), may hold values from -6 to 6
- gate_logits: bfloat16 [1, 16384, 8192], P(None, 'ctx', ('dp', 'pipe')), may hold values from -6 to 6
- cotangent: bfloat16 [1, 16384, 8192], P(None, 'ctx', ('dp', 'pipe')), may hold values from -6 to 6
- decay_rates: float32 [64], P(('dp', 'pipe')), may hold values from 3.0517578e-05 to 0.05
- norm_gain: float32 [64, 128], P(('dp', 'pipe')), may hold values from 0.5 to 1.5
- block_starts: int32 [1, 64], P(None, 'ctx'), may hold values 0 or 1
Outputs:
- mixed_out: bfloat16 [1, 16384, 8192], P(None, 'ctx', ('dp', 'pipe'))
- query_grad: bfloat16 [1, 16384, 8192], P(None, 'ctx', ('dp', 'pipe'))
- key_grad: bfloat16 [1, 16384, 8192], P(None, 'ctx', ('dp', 'pipe'))
- value_grad: bfloat16 [1, 16384, 8192], P(None, 'ctx', ('dp', 'pipe'))
- gate_grad: bfloat16 [1, 16384, 8192], P(None, 'ctx', ('dp', 'pipe'))
- gain_grad: float32 [64, 128], P(('dp', 'pipe'))
The draws below stay inside these ranges and needn't reach their ends.
All inputs are finite; a program needn't handle non-finite values. No bound on the sum of `block_starts` on one device may be relied on, other than what follows from the above.
Results may differ from the reference program's by a relative error of at most 0.0012.
Values sent between devices are 32-bit elements; how exact they have to be, the bound alone decides.
No kernel may reach another device: no remote copies, remote signals or barrier semaphores. Data moves between devices by JAX's collectives and lax.ppermute only.
A program may use at most 32 MiB of HBM per device.

```python
import math
import jax
import jax.numpy as jnp
from jax import lax

HEADS = 64
DH = 128
BLOCK = 256
BATCH = 1
SEQ = 16384
BLOCKS = 64
FEAT = 8192


def plant(drawn, stream_key, low, high):
    longest = drawn.shape.index(max(drawn.shape))
    spots = []
    for shift in (0, 1):
        where = [jax.random.randint(jax.random.fold_in(stream_key, axis), (), 0, length) for axis, length in enumerate(drawn.shape)]
        where[longest] = (where[longest] + shift) % drawn.shape[longest]
        spots.append(tuple(where))
    return drawn.at[spots[0]].set(low).at[spots[1]].set(high)


def shard_levels(own_key, extent, cuts, least, high):
    def one(position, shards_of):
        steps = jax.random.uniform(jax.random.fold_in(jax.random.fold_in(own_key, 6), position), (shards_of,), jnp.float32, least / len(cuts), high / len(cuts))
        return jnp.repeat(jnp.exp(steps), extent[position] // shards_of).reshape((-1,) + (1,) * (len(extent) - position - 1))

    level = one(*cuts[0])
    for cut in cuts[1:]:
        level = level * one(*cut)
    return level


def centred(rng, dims, scale, most, cuts=(), kind=jnp.bfloat16):
    drawn = scale * jax.random.normal(rng, dims, jnp.float32)
    if cuts:
        drawn = drawn * shard_levels(rng, dims, cuts, -0.22, 0.18)
    return jnp.clip(drawn, -most, most).astype(kind)


def setup_inputs(seed: int = 0) -> dict:
    key_list = jax.random.split(jax.random.key(seed), 9)
    return {
        "queries": centred(key_list[0], (BATCH, SEQ, FEAT), 0.3, 2.0, ((1, 16), (2, 64))),
        "key_tokens": centred(key_list[1], (BATCH, SEQ, FEAT), 0.3, 2.0, ((1, 16), (2, 64))),
        "values": centred(key_list[2], (BATCH, SEQ, FEAT), 1.0, 6.0, ((1, 16), (2, 64))),
        "gate_logits": centred(key_list[3], (BATCH, SEQ, FEAT), 1.0, 6.0, ((1, 16), (2, 64))),
        "cotangent": centred(key_list[4], (BATCH, SEQ, FEAT), 1.0, 6.0, ((1, 16), (2, 64))),
        "decay_rates": jnp.clip(jnp.exp(math.log(0.05) - 7.4014754 * jax.random.uniform(key_list[5], (HEADS,), jnp.float32) ** shard_levels(key_list[5], (HEADS,), ((0, 64),), -0.2, 0.2)), 3.0517578125e-05, 0.05),
        "norm_gain": jnp.clip(1.0 + 0.1 * jax.random.normal(key_list[6], (HEADS, DH), jnp.float32), 0.5, 1.5),
        "block_starts": plant((jax.random.randint(key_list[7], (BATCH, BLOCKS), 0, 4) < 1).astype(jnp.int32), jax.random.fold_in(key_list[7], 1), 0, 1),
    }


highest = lax.Precision.HIGHEST
epsilon = 1e-06

def run_blocks(query_rows, key_rows, value_rows, decay_rate, block_flags, block_size):
    block_count = query_rows.shape[0] // block_size
    query_blocks = query_rows.reshape(block_count, block_size, -1)
    key_blocks = key_rows.reshape(block_count, block_size, -1)
    value_blocks = value_rows.reshape(block_count, block_size, -1)
    offsets = jnp.arange(block_size, dtype=jnp.float32)
    distance = offsets[:, None] - offsets[None, :]
    weights = jnp.where(distance >= 0, jnp.exp(-decay_rate * jnp.maximum(distance, 0.0)), 0.0)
    decay_in = jnp.exp(-decay_rate * offsets)
    decay_out = jnp.exp(-decay_rate * (block_size - offsets))
    decay_block = jnp.exp(-decay_rate * block_size)

    def advance(carried, pieces):
        query_part, key_part, value_part, flag = pieces
        carried = carried * (1.0 - flag)
        scores = jnp.dot(query_part, key_part.T, precision=highest) * weights
        result = jnp.dot(scores, value_part, precision=highest) + decay_in[:, None] * jnp.dot(query_part, carried, precision=highest)
        carried = decay_block * carried + jnp.dot(key_part.T, decay_out[:, None] * value_part, precision=highest)
        return (carried, result)
    initial = jnp.zeros((key_rows.shape[1], value_rows.shape[1]), jnp.float32)
    closing, results = lax.scan(advance, initial, (query_blocks, key_blocks, value_blocks, block_flags))
    return (results.reshape(query_rows.shape[0], -1), closing)

def to_heads(array):
    return array.astype(jnp.float32).reshape(SEQ, HEADS, DH).transpose(1, 0, 2)

def from_heads(array):
    return array.transpose(1, 0, 2).reshape(SEQ, HEADS * DH)

def flipped(array):
    return jnp.flip(array, axis=1)

def reference(queries, key_tokens, values, gate_logits, cotangent, decay_rates, norm_gain, block_starts):
    gain_flat = norm_gain.reshape(-1)

    def one_sequence(pieces):
        query_in, key_in, value_in, gate_in, grad_in, starts_in = pieces
        start_flags = starts_in.astype(jnp.float32)
        reverse_flags = jnp.flip(jnp.concatenate([start_flags[1:], jnp.zeros((1,), jnp.float32)]))

        def forward_run(query_rows, key_rows, value_rows, decay_rate):
            return run_blocks(query_rows, key_rows, value_rows, decay_rate, start_flags, BLOCK)[0]

        def backward_run(query_rows, key_rows, value_rows, decay_rate):
            return run_blocks(query_rows, key_rows, value_rows, decay_rate, reverse_flags, BLOCK)[0]
        forward_many = jax.vmap(forward_run)
        backward_many = jax.vmap(backward_run)
        query_heads = to_heads(query_in)
        key_heads = to_heads(key_in)
        value_heads = to_heads(value_in)
        mixed = from_heads(forward_many(query_heads, key_heads, value_heads, decay_rates))
        gate_open = jax.nn.sigmoid(gate_in.astype(jnp.float32))
        grad_out = grad_in.astype(jnp.float32)
        grad_norm = grad_out * gate_open * gain_flat
        sq_sum = lax.optimization_barrier(jnp.sum(mixed * mixed, axis=1))
        cross_dot = lax.optimization_barrier(jnp.sum(grad_norm * mixed, axis=1))
        inverse = lax.rsqrt(sq_sum / FEAT + epsilon)
        normed = mixed * inverse[:, None]
        mixed_out = (gate_open * gain_flat * normed).astype(jnp.bfloat16)
        gate_grad = (grad_out * gain_flat * normed * gate_open * (1.0 - gate_open)).astype(jnp.bfloat16)
        grad_mixed = inverse[:, None] * (grad_norm - normed * (inverse * cross_dot / FEAT)[:, None])
        grad_heads = to_heads(grad_mixed)
        query_grad = from_heads(forward_many(grad_heads, value_heads, key_heads, decay_rates)).astype(jnp.bfloat16)
        value_grad = from_heads(flipped(backward_many(flipped(key_heads), flipped(query_heads), flipped(grad_heads), decay_rates))).astype(jnp.bfloat16)
        key_grad = from_heads(flipped(backward_many(flipped(value_heads), flipped(grad_heads), flipped(query_heads), decay_rates))).astype(jnp.bfloat16)
        gain_part = lax.optimization_barrier(jnp.sum(grad_out * gate_open * normed, axis=0))
        return (mixed_out, query_grad, key_grad, value_grad, gate_grad, gain_part)
    mixed_out, query_grad, key_grad, value_grad, gate_grad, gain_parts = lax.map(one_sequence, (queries, key_tokens, values, gate_logits, cotangent, block_starts))
    gain_grad = (lax.optimization_barrier(jnp.sum(gain_parts, axis=0)) / math.sqrt(BATCH * SEQ)).reshape(HEADS, DH)
    return (mixed_out, query_grad, key_grad, value_grad, gate_grad, gain_grad)
```

```python
import math

import jax
import jax.numpy as jnp
from jax import lax
from jax.experimental import pallas as pl
from jax.experimental.pallas import tpu as pltpu
from jax.sharding import PartitionSpec as P

BLOCK = 256
EPSILON = 1e-06
F32 = jnp.float32
BF16 = jnp.bfloat16
WIDTH = 128
HALF = 64
LIMIT = 24 << 20


def split(x):
    high = x.astype(BF16)
    return high, (x - high.astype(F32)).astype(BF16)


def dot(a, b, da=1, db=0):
    return lax.dot_general(a, b, (((da,), (db,)), ((), ())), preferred_element_type=F32)


def dot_split(a, x, da=1):
    high, low = split(x)
    both = dot(a, jnp.concatenate([high, low], axis=1), da, 0)
    n = x.shape[1]
    return both[:, :n] + both[:, n:]


def rows_iota(rows, columns=WIDTH):
    return lax.broadcasted_iota(jnp.int32, (rows, columns), 0).astype(F32)


def decay_matrix(rate):
    at = lax.broadcasted_iota(jnp.int32, (BLOCK, BLOCK), 0)
    of = lax.broadcasted_iota(jnp.int32, (BLOCK, BLOCK), 1)
    distance = (at - of).astype(F32)
    return jnp.where(distance >= 0, jnp.exp(-rate * jnp.maximum(distance, 0.0)), 0.0)


def power(rate, tokens):
    return jnp.exp(jnp.full((1, WIDTH), -rate * tokens, F32))


def block_rows(b):
    return pl.ds(b * BLOCK, BLOCK)


def kept(flags_ref, b):
    return 1.0 - flags_ref[0, b].astype(F32)


def closing_kernel(rate_ref, flags_ref, k_ref, v_ref, own_ref, pairs_ref):
    rate = rate_ref[0]
    blocks = k_ref.shape[1] // BLOCK
    decay_out = jnp.exp(-rate * (float(BLOCK) - rows_iota(BLOCK)))
    over_block = power(rate, float(BLOCK))
    carried = jnp.zeros((WIDTH, WIDTH), F32)
    unbroken = 1.0
    for b in range(blocks):
        keep = kept(flags_ref, b)
        piece = dot_split(
            k_ref[0, block_rows(b)], decay_out * v_ref[0, block_rows(b)].astype(F32), 0
        )
        pairs_ref[b] = piece
        carried = carried * (over_block * keep) + piece
        unbroken = unbroken * keep
    own_ref[:WIDTH] = carried
    own_ref[WIDTH:] = jnp.full((8, WIDTH), unbroken, F32)


def local_kernel(rate_ref, q_ref, k_ref, v_ref, out_ref):
    weights = decay_matrix(rate_ref[0])
    for b in range(q_ref.shape[1] // BLOCK):
        rows = block_rows(b)
        scores = dot(q_ref[0, rows], k_ref[0, rows], 1, 1) * weights
        high, low = split(scores)
        v = v_ref[0, rows]
        out_ref[rows] = dot(high, v) + dot(low, v)


def forward_half_kernel(tokens, rate_ref, place_ref, own_ref, other_ref, out_ref):
    second = lax.rem(place_ref[0], 2) == 1
    over_slab = power(rate_ref[0], float(tokens))
    own, other = own_ref[:WIDTH], other_ref[:WIDTH]
    early = jnp.where(second, other, own)
    late = jnp.where(second, own, other)
    late_kept = jnp.where(second, own_ref[WIDTH : WIDTH + 1], other_ref[WIDTH : WIDTH + 1])
    chip = early * (late_kept * over_slab) + late
    out_ref[:HALF] = jnp.where(second, chip[HALF:], chip[:HALF])
    out_ref[HALF:] = own_ref[WIDTH:]


def backward_half_kernel(tokens, rate_ref, place_ref, own_ref, other_ref, gain_ref, unbroken_ref, out_ref):
    place = place_ref[0]
    second = lax.rem(place, 2) == 1
    over_slab = power(rate_ref[0], float(tokens))
    own, other = own_ref[...], other_ref[...]
    early = jnp.where(second, other, own)
    late = jnp.where(second, own, other)
    early_kept = unbroken_ref[pl.ds(place - lax.rem(place, 2), 1)]
    chip = late * (early_kept * over_slab) + early
    out_ref[:HALF] = jnp.where(second, chip[HALF:], chip[:HALF])
    out_ref[HALF:] = jnp.broadcast_to(gain_ref[...], (8, WIDTH))


def chip_state(all_ref, c):
    return jnp.concatenate([all_ref[2 * c, :HALF], all_ref[2 * c + 1, :HALF]], axis=0)


def attended_kernel(
    tokens,
    rate_ref,
    flags_ref,
    place_ref,
    all_ref,
    other_ref,
    pairs_ref,
    q_ref,
    local_ref,
    gate_ref,
    cotangent_ref,
    gain_ref,
    attended_ref,
    states_ref,
    sums_ref,
    unbroken_ref,
):
    rate = rate_ref[0]
    place = place_ref[0]
    chip, core = place // 2, lax.rem(place, 2)
    over_slab = power(rate, float(tokens))
    slabs = all_ref.shape[0]
    state = jnp.zeros((WIDTH, WIDTH), F32)
    for c in range(slabs // 2):
        before = c < chip
        factor = all_ref[2 * c, HALF : HALF + 1] * all_ref[2 * c + 1, HALF : HALF + 1]
        state = jnp.where(
            before, state * (factor * over_slab * over_slab) + chip_state(all_ref, c), state
        )
    state = jnp.where(
        core == 1,
        state * (other_ref[WIDTH : WIDTH + 1] * over_slab) + other_ref[:WIDTH],
        state,
    )
    for s in range(slabs):
        unbroken_ref[s : s + 1] = all_ref[s, HALF : HALF + 1]
    decay_in = jnp.exp(-rate * rows_iota(BLOCK))
    over_block = power(rate, float(BLOCK))
    ones = jnp.ones((8, WIDTH), BF16)
    first = lax.broadcasted_iota(jnp.int32, (8, BLOCK), 0) == 0
    for b in range(tokens // BLOCK):
        rows = block_rows(b)
        state = state * kept(flags_ref, b)
        states_ref[b] = state
        attended = local_ref[rows] + decay_in * dot_split(q_ref[0, rows], state)
        attended_ref[rows] = attended
        opening = jax.nn.sigmoid(gate_ref[0, rows].astype(F32))
        grad_norm = cotangent_ref[0, rows].astype(F32) * opening * gain_ref[...]
        sq_high, sq_low = split(attended * attended)
        cross_high, cross_low = split(grad_norm * attended)
        squares = dot(ones, sq_high, 1, 1) + dot(ones, sq_low, 1, 1)
        crosses = dot(ones, cross_high, 1, 1) + dot(ones, cross_low, 1, 1)
        both = jnp.where(first, squares, crosses)[:2]
        for p in range(sums_ref.shape[0]):
            sums_ref[p, :, b * BLOCK : (b + 1) * BLOCK] = both
        state = state * over_block + pairs_ref[b]


def spread_kernel(parts_ref, out_ref):
    total = parts_ref[0]
    for p in range(1, parts_ref.shape[0]):
        total = total + parts_ref[p]
    for p in range(out_ref.shape[0]):
        out_ref[p] = total


def thirds(row):
    high = row.astype(BF16).astype(F32)
    rest = row - high
    middle = rest.astype(BF16).astype(F32)
    return high, middle, rest - middle


def columns_of(first, second):
    pieces = thirds(first) + thirds(second)
    n = first.shape[1]
    at = lax.broadcasted_iota(jnp.int32, (16, n), 0)
    stacked = jnp.zeros((16, n), F32)
    for i, piece in enumerate(pieces):
        stacked = jnp.where(at == i, piece, stacked)
    row = lax.broadcasted_iota(jnp.int32, (16, 2 * WIDTH), 0)
    column = lax.broadcasted_iota(jnp.int32, (16, 2 * WIDTH), 1)
    chosen = jnp.where((row >= 3) == (column >= WIDTH), 1.0, 0.0).astype(BF16)
    both = dot(stacked.astype(BF16), chosen, 0, 0)
    return both[:, :WIDTH], both[:, WIDTH:]


def grad_kernel(
    features,
    row_total,
    rate_ref,
    flags_ref,
    parts_ref,
    attended_ref,
    q_ref,
    gate_ref,
    cotangent_ref,
    gain_ref,
    own_ref,
    gain_part_ref,
    high_ref,
    low_ref,
    pieces_ref,
    inverse_ref,
):
    rate = rate_ref[0]
    total = parts_ref[0]
    for p in range(1, parts_ref.shape[0]):
        total = total + parts_ref[p]
    inverse_row = lax.rsqrt(total[0:1] * (1.0 / features) + EPSILON)
    slope_row = inverse_row * total[1:2] * (1.0 / features)
    decay_on = jnp.exp(-rate * (rows_iota(BLOCK) + 1.0))
    over_block = power(rate, float(BLOCK))
    carried = jnp.zeros((WIDTH, WIDTH), F32)
    gain_sum = jnp.zeros((1, WIDTH), F32)
    for b in reversed(range(q_ref.shape[1] // BLOCK)):
        rows = block_rows(b)
        lanes = slice(b * BLOCK, (b + 1) * BLOCK)
        inverse, slope = columns_of(inverse_row[:, lanes], slope_row[:, lanes])
        inverse_ref[rows] = inverse
        normed = attended_ref[rows] * inverse
        opening = jax.nn.sigmoid(gate_ref[0, rows].astype(F32))
        grad_open = cotangent_ref[0, rows].astype(F32) * opening
        gain_sum = gain_sum + jnp.sum(grad_open * normed, axis=0, keepdims=True)
        grad = inverse * (grad_open * gain_ref[...] - normed * slope)
        high, low = split(grad)
        high_ref[rows] = high
        low_ref[rows] = low
        piece = dot_split(q_ref[0, rows], decay_on * grad, 0)
        pieces_ref[b] = piece
        carried = (carried * over_block + piece) * kept(flags_ref, b)
    own_ref[...] = carried
    gain_part_ref[...] = gain_sum * (1.0 / math.sqrt(row_total))


def backward_kernel(
    rate_ref,
    q_ref,
    k_ref,
    v_ref,
    gate_ref,
    cotangent_ref,
    gain_ref,
    high_ref,
    low_ref,
    inverse_ref,
    attended_ref,
    states_ref,
    mixed_ref,
    gate_grad_ref,
    query_grad_ref,
    key_part_ref,
    value_part_ref,
):
    rate = rate_ref[0]
    weights = decay_matrix(rate)
    decay_in = jnp.exp(-rate * rows_iota(BLOCK))
    for b in range(q_ref.shape[1] // BLOCK):
        rows = block_rows(b)
        q, k, v = q_ref[0, rows], k_ref[0, rows], v_ref[0, rows]
        high, low = high_ref[rows], low_ref[rows]
        normed = attended_ref[rows] * inverse_ref[rows]
        opening = jax.nn.sigmoid(gate_ref[0, rows].astype(F32))
        mixed = opening * gain_ref[...] * normed
        mixed_ref[0, rows] = mixed.astype(BF16)
        gate_grad_ref[0, rows] = (
            cotangent_ref[0, rows].astype(F32) * mixed * (1.0 - opening)
        ).astype(BF16)
        slopes = (dot(high, v, 1, 1) + dot(low, v, 1, 1)) * weights
        slopes_high, slopes_low = split(slopes)
        state_high, state_low = split(states_ref[b])
        across = dot(high, state_high, 1, 1) + dot(high, state_low, 1, 1) + dot(low, state_high, 1, 1)
        query_grad_ref[0, rows] = (
            dot(slopes_high, k) + dot(slopes_low, k) + decay_in * across
        ).astype(BF16)
        key_part_ref[rows] = dot(slopes_high, q, 0, 0) + dot(slopes_low, q, 0, 0)
        scores_high, scores_low = split(dot(q, k, 1, 1) * weights)
        both = dot(scores_high, jnp.concatenate([high, low], axis=1), 0, 0)
        value_part_ref[rows] = both[:, :WIDTH] + both[:, WIDTH:] + dot(scores_low, high, 0, 0)


def finish_kernel(
    tokens,
    rate_ref,
    flags_ref,
    place_ref,
    all_ref,
    other_ref,
    unbroken_ref,
    pieces_ref,
    k_ref,
    v_ref,
    key_part_ref,
    value_part_ref,
    key_grad_ref,
    value_grad_ref,
    gain_grad_ref,
):
    rate = rate_ref[0]
    place = place_ref[0]
    chip, core = place // 2, lax.rem(place, 2)
    over_slab = power(rate, float(tokens))
    slabs = all_ref.shape[0]
    state = jnp.zeros((WIDTH, WIDTH), F32)
    for c in reversed(range(slabs // 2)):
        after = c > chip
        factor = unbroken_ref[2 * c : 2 * c + 1] * unbroken_ref[2 * c + 1 : 2 * c + 2]
        state = jnp.where(
            after, state * (factor * over_slab * over_slab) + chip_state(all_ref, c), state
        )
    partner = unbroken_ref[pl.ds(place - core + 1, 1)]
    state = jnp.where(core == 0, state * (partner * over_slab) + other_ref[...], state)
    gain = all_ref[0, HALF : HALF + 1]
    for s in range(1, slabs):
        gain = gain + all_ref[s, HALF : HALF + 1]
    gain_grad_ref[...] = gain
    decay_back = jnp.exp(-rate * (float(BLOCK - 1) - rows_iota(BLOCK)))
    over_block = power(rate, float(BLOCK))
    last = tokens // BLOCK - 1
    for b in reversed(range(last + 1)):
        rows = block_rows(b)
        if b < last:
            state = state * kept(flags_ref, b + 1)
        high, low = split(state)
        k, v = k_ref[0, rows], v_ref[0, rows]
        both = dot(k, jnp.concatenate([high, low], axis=1))
        value_grad_ref[0, rows] = (
            value_part_ref[rows] + decay_back * (both[:, :WIDTH] + both[:, WIDTH:])
        ).astype(BF16)
        both = dot(v, jnp.concatenate([high, low], axis=0), 1, 1)
        key_grad_ref[0, rows] = (
            key_part_ref[rows] + decay_back * (both[:, :WIDTH] + both[:, WIDTH:])
        ).astype(BF16)
        state = state * over_block + pieces_ref[b]


def call(kernel, scalars, arrays, outs, flops=1 << 24):
    smem = pl.BlockSpec(memory_space=pltpu.SMEM)
    vmem = pl.BlockSpec(memory_space=pltpu.VMEM)
    moved = sum(a.size * a.dtype.itemsize for a in (*arrays, *outs))
    return pl.pallas_call(
        kernel,
        out_shape=outs,
        in_specs=[smem] * len(scalars) + [vmem] * len(arrays),
        out_specs=[vmem] * len(outs),
        compiler_params=pltpu.CompilerParams(vmem_limit_bytes=LIMIT),
        cost_estimate=pl.CostEstimate(flops=flops, bytes_accessed=moved, transcendentals=0),
    )(*scalars, *arrays)


def shape(*dims, dtype=F32):
    return jax.ShapeDtypeStruct(dims, dtype)


def bound(kernel, *fixed):
    def run(*refs):
        kernel(*fixed, *refs)

    return run


def body(queries, key_tokens, values, gate_logits, cotangent, decay_rates, norm_gain, block_starts):
    tokens = queries.shape[1]
    blocks = tokens // BLOCK
    slabs = lax.axis_size("ctx")
    outer, inner = lax.axis_size("dp"), lax.axis_size("pipe")
    features = float(WIDTH * outer * inner)
    place = lax.axis_index("ctx").astype(jnp.int32).reshape(1)
    partners = [(j, j ^ 1) for j in range(slabs)]
    like = shape(1, tokens, WIDTH, dtype=BF16)
    wide = shape(tokens, WIDTH)
    states = shape(blocks, WIDTH, WIDTH)

    own, pairs = call(
        closing_kernel,
        (decay_rates, block_starts),
        (key_tokens, values),
        [shape(WIDTH + 8, WIDTH), states],
    )
    other = lax.ppermute(own, "ctx", partners)
    (local,) = call(
        local_kernel, (decay_rates,), (queries, key_tokens, values), [wide], flops=1 << 28
    )
    (half,) = call(
        bound(forward_half_kernel, tokens),
        (decay_rates, place),
        (own, other),
        [shape(HALF + 8, WIDTH)],
    )
    everyone = lax.all_gather(half, "ctx")
    attended, states_in, sums, unbroken = call(
        bound(attended_kernel, tokens),
        (decay_rates, block_starts, place),
        (everyone, other, pairs, queries, local, gate_logits, cotangent, norm_gain),
        [wide, states, shape(inner, 2, tokens), shape(slabs, WIDTH)],
    )
    sums = lax.all_to_all(sums, "pipe", 0, 0, tiled=True)
    (sums,) = call(spread_kernel, (), (sums,), [shape(outer, 2, tokens)])
    sums = lax.all_to_all(sums, "dp", 0, 0, tiled=True)
    back, gain_part, high, low, pieces, inverse = call(
        bound(grad_kernel, features, tokens * slabs),
        (decay_rates, block_starts),
        (sums, attended, queries, gate_logits, cotangent, norm_gain),
        [
            shape(WIDTH, WIDTH),
            shape(1, WIDTH),
            shape(tokens, WIDTH, dtype=BF16),
            shape(tokens, WIDTH, dtype=BF16),
            states,
            wide,
        ],
    )
    back_other = lax.ppermute(back, "ctx", partners)
    mixed_out, gate_grad, query_grad, key_part, value_part = call(
        backward_kernel,
        (decay_rates,),
        (
            queries,
            key_tokens,
            values,
            gate_logits,
            cotangent,
            norm_gain,
            high,
            low,
            inverse,
            attended,
            states_in,
        ),
        [like, like, like, wide, wide],
        flops=1 << 30,
    )
    (back_half,) = call(
        bound(backward_half_kernel, tokens),
        (decay_rates, place),
        (back, back_other, gain_part, unbroken),
        [shape(HALF + 8, WIDTH)],
    )
    back_everyone = lax.all_gather(back_half, "ctx")
    key_grad, value_grad, gain_grad = call(
        bound(finish_kernel, tokens),
        (decay_rates, block_starts, place),
        (
            back_everyone,
            back_other,
            unbroken,
            pieces,
            key_tokens,
            values,
            key_part,
            value_part,
        ),
        [like, like, shape(1, WIDTH)],
    )
    return (mixed_out, query_grad, key_grad, value_grad, gate_grad, gain_grad)


def solution(mesh):
    wide = P(None, "ctx", ("dp", "pipe"))
    heads = P(("dp", "pipe"))
    gain = P(("dp", "pipe"), None)
    return jax.shard_map(
        body,
        mesh=mesh,
        in_specs=(wide, wide, wide, wide, wide, heads, gain, P(None, "ctx")),
        out_specs=(wide, wide, wide, wide, wide, gain),
        check_vma=False,
    )
```

```python
import math

import jax
import jax.numpy as jnp
from jax import lax
from jax.experimental import pallas as pl
from jax.experimental.pallas import tpu as pltpu
from jax.sharding import PartitionSpec as P

BLOCK = 256
EPSILON = 1e-06
F32 = jnp.float32
BF16 = jnp.bfloat16
WIDTH = 128
HALF = 64
LIMIT = 12 << 20


def split(x):
    high = x.astype(BF16)
    return high, (x - high.astype(F32)).astype(BF16)


def dot(a, b, da=1, db=0):
    return lax.dot_general(a, b, (((da,), (db,)), ((), ())), preferred_element_type=F32)


def dot_split(a, x, da=1):
    high, low = split(x)
    both = dot(a, jnp.concatenate([high, low], axis=1), da, 0)
    n = x.shape[1]
    return both[:, :n] + both[:, n:]


def rows_iota(rows, columns=WIDTH):
    return lax.broadcasted_iota(jnp.int32, (rows, columns), 0).astype(F32)


def power(facts_ref, tokens):
    return jnp.exp(-rate_row(facts_ref) * tokens)


def rate_row(facts_ref):
    return facts_ref[0:1, :WIDTH]


def kept(facts_ref, b):
    return facts_ref[b + 1 : b + 2, :WIDTH]


def block_rows(b):
    return pl.ds(b * BLOCK, BLOCK)


def decay_matrix(facts_ref, at_axis=0):
    at = lax.broadcasted_iota(jnp.int32, (BLOCK, BLOCK), at_axis)
    of = lax.broadcasted_iota(jnp.int32, (BLOCK, BLOCK), 1 - at_axis)
    distance = (at - of).astype(F32)
    return jnp.where(
        distance >= 0, jnp.exp(-facts_ref[0:1] * jnp.maximum(distance, 0.0)), 0.0
    )


def halves(both):
    return both[:, :WIDTH] + both[:, WIDTH:]


def beside(a, b):
    return jnp.concatenate([a, b], axis=1)


def closing_kernel(
    rate_ref,
    flags_hbm,
    k_hbm,
    v_hbm,
    q_hbm,
    gain_hbm,
    own_ref,
    pairs_ref,
    facts_ref,
    k_ref,
    v_ref,
    q_ref,
    gain_ref,
    flags_smem,
    sems,
):
    blocks = k_ref.shape[0] // BLOCK
    flags_copy = pltpu.make_async_copy(flags_hbm, flags_smem, sems.at[0])
    flags_copy.start()
    parts = []
    for b in range(blocks):
        rows = block_rows(b)
        parts.append(
            [
                pltpu.make_async_copy(k_hbm.at[0, rows], k_ref.at[rows], sems.at[1 + 2 * b]),
                pltpu.make_async_copy(v_hbm.at[0, rows], v_ref.at[rows], sems.at[2 + 2 * b]),
            ]
        )
        for copy in parts[b]:
            copy.start()
    at = 1 + 2 * blocks
    rest = [
        pltpu.make_async_copy(q_hbm.at[0], q_ref, sems.at[at]),
        pltpu.make_async_copy(gain_hbm, gain_ref, sems.at[at + 1]),
    ]
    for copy in rest:
        copy.start()
    flags_copy.wait()
    facts_ref[0:1] = jnp.full((1, BLOCK), rate_ref[0], F32)
    unbroken = 1.0
    for b in range(blocks):
        keep = 1.0 - flags_smem[0, b].astype(F32)
        unbroken = unbroken * keep
        facts_ref[b + 1 : b + 2] = jnp.full((1, BLOCK), keep, F32)
    decay_out = jnp.exp(-rate_row(facts_ref) * (float(BLOCK) - rows_iota(BLOCK)))
    over_block = power(facts_ref, float(BLOCK))
    carried = jnp.zeros((WIDTH, WIDTH), F32)
    for b in range(blocks):
        for copy in parts[b]:
            copy.wait()
        rows = block_rows(b)
        piece = dot_split(k_ref[rows], decay_out * v_ref[rows].astype(F32), 0)
        pairs_ref[b] = piece
        carried = carried * (over_block * kept(facts_ref, b)) + piece
    own_ref[:WIDTH] = carried
    own_ref[WIDTH:] = jnp.full((8, WIDTH), unbroken, F32)
    for copy in rest:
        copy.wait()


def local_kernel(facts_ref, q_ref, k_ref, v_ref, out_ref):
    weights = decay_matrix(facts_ref)
    for b in range(q_ref.shape[0] // BLOCK):
        rows = block_rows(b)
        scores = dot(q_ref[rows], k_ref[rows], 1, 1) * weights
        high, low = split(scores)
        v = v_ref[rows]
        out_ref[rows] = dot(high, v) + dot(low, v)


def forward_half_kernel(tokens, place_ref, facts_ref, own_ref, other_ref, out_ref):
    second = lax.rem(place_ref[0], 2) == 1
    over_slab = power(facts_ref, float(tokens))
    own, other = own_ref[:WIDTH], other_ref[:WIDTH]
    early = jnp.where(second, other, own)
    late = jnp.where(second, own, other)
    late_kept = jnp.where(second, own_ref[WIDTH : WIDTH + 1], other_ref[WIDTH : WIDTH + 1])
    chip = early * (late_kept * over_slab) + late
    out_ref[:HALF] = jnp.where(second, chip[HALF:], chip[:HALF])
    out_ref[HALF:] = own_ref[WIDTH:]


def backward_half_kernel(
    tokens, place_ref, facts_ref, own_ref, other_ref, gain_ref, unbroken_ref, out_ref
):
    place = place_ref[0]
    second = lax.rem(place, 2) == 1
    over_slab = power(facts_ref, float(tokens))
    own, other = own_ref[...], other_ref[...]
    early = jnp.where(second, other, own)
    late = jnp.where(second, own, other)
    early_kept = unbroken_ref[pl.ds(place - lax.rem(place, 2), 1)]
    chip = late * (early_kept * over_slab) + early
    out_ref[:HALF] = jnp.where(second, chip[HALF:], chip[:HALF])
    out_ref[HALF:] = jnp.broadcast_to(gain_ref[...], (8, WIDTH))


def chip_state(all_ref, c):
    return jnp.concatenate([all_ref[2 * c, :HALF], all_ref[2 * c + 1, :HALF]], axis=0)


def attended_kernel(
    tokens,
    place_ref,
    facts_ref,
    all_ref,
    other_ref,
    pairs_ref,
    q_ref,
    local_ref,
    gate_ref,
    cotangent_ref,
    gain_ref,
    attended_ref,
    states_ref,
    sums_ref,
    unbroken_ref,
):
    place = place_ref[0]
    chip, core = place // 2, lax.rem(place, 2)
    over_slab = power(facts_ref, float(tokens))
    slabs = all_ref.shape[0]
    state = jnp.zeros((WIDTH, WIDTH), F32)
    for c in range(slabs // 2):
        before = c < chip
        factor = all_ref[2 * c, HALF : HALF + 1] * all_ref[2 * c + 1, HALF : HALF + 1]
        state = jnp.where(
            before, state * (factor * over_slab * over_slab) + chip_state(all_ref, c), state
        )
    state = jnp.where(
        core == 1,
        state * (other_ref[WIDTH : WIDTH + 1] * over_slab) + other_ref[:WIDTH],
        state,
    )
    for s in range(slabs):
        unbroken_ref[s : s + 1] = all_ref[s, HALF : HALF + 1]
    decay_in = jnp.exp(-rate_row(facts_ref) * rows_iota(BLOCK))
    over_block = power(facts_ref, float(BLOCK))
    ones = jnp.ones((8, 2 * WIDTH), BF16)
    first = lax.broadcasted_iota(jnp.int32, (8, BLOCK), 0) == 0
    for b in range(tokens // BLOCK):
        rows = block_rows(b)
        state = state * kept(facts_ref, b)
        states_ref[b] = state
        attended = local_ref[rows] + decay_in * dot_split(q_ref[rows], state)
        attended_ref[rows] = attended
        opening = jax.nn.sigmoid(gate_ref[rows].astype(F32))
        grad_norm = cotangent_ref[rows].astype(F32) * opening * gain_ref[...]
        squares = dot(ones, beside(*split(attended * attended)), 1, 1)
        crosses = dot(ones, beside(*split(grad_norm * attended)), 1, 1)
        both = jnp.where(first, squares, crosses)[:2]
        for p in range(sums_ref.shape[0]):
            sums_ref[p, :, b * BLOCK : (b + 1) * BLOCK] = both
        state = state * over_block + pairs_ref[b]


def spread_kernel(parts_ref, out_ref):
    total = parts_ref[0]
    for p in range(1, parts_ref.shape[0]):
        total = total + parts_ref[p]
    for p in range(out_ref.shape[0]):
        out_ref[p] = total


def beforehand_kernel(
    facts_ref,
    k_ref,
    v_ref,
    gate_ref,
    cotangent_ref,
    gain_ref,
    attended_ref,
    states_ref,
    query_ref,
):
    weights = decay_matrix(facts_ref)
    decay_in = jnp.exp(-rate_row(facts_ref) * rows_iota(BLOCK))
    for b in range(k_ref.shape[0] // BLOCK):
        rows = block_rows(b)
        k, v = k_ref[rows], v_ref[rows]
        opening = jax.nn.sigmoid(gate_ref[rows].astype(F32))
        grad_norm = cotangent_ref[rows].astype(F32) * opening * gain_ref[...]
        twice = beside(v, v)
        state_high, state_low = split(states_ref[b])
        state_twice = beside(state_high, state_high)
        for i, left in enumerate((grad_norm, attended_ref[rows])):
            high, low = split(left)
            both = beside(high, low)
            across = dot(both, state_twice, 1, 1) + dot(high, state_low, 1, 1)
            high, low = split(dot(both, twice, 1, 1) * weights)
            query_ref[i, rows] = dot(high, k) + dot(low, k) + decay_in * across


def thirds(row):
    high = row.astype(BF16).astype(F32)
    rest = row - high
    middle = rest.astype(BF16).astype(F32)
    return high, middle, rest - middle


def columns_of(first, second):
    pieces = thirds(first) + thirds(second)
    n = first.shape[1]
    at = lax.broadcasted_iota(jnp.int32, (16, n), 0)
    stacked = jnp.zeros((16, n), F32)
    for i, piece in enumerate(pieces):
        stacked = jnp.where(at == i, piece, stacked)
    row = lax.broadcasted_iota(jnp.int32, (16, 2 * WIDTH), 0)
    column = lax.broadcasted_iota(jnp.int32, (16, 2 * WIDTH), 1)
    chosen = jnp.where((row >= 3) == (column >= WIDTH), 1.0, 0.0).astype(BF16)
    both = dot(stacked.astype(BF16), chosen, 0, 0)
    return both[:, :WIDTH], both[:, WIDTH:]


def grad_kernel(
    features,
    row_total,
    facts_ref,
    parts_ref,
    attended_ref,
    q_ref,
    gate_ref,
    cotangent_ref,
    gain_ref,
    query_ref,
    own_ref,
    gain_part_ref,
    grad_ref,
    pieces_ref,
    mixed_ref,
    gate_grad_ref,
    query_grad_ref,
):
    total = parts_ref[0]
    for p in range(1, parts_ref.shape[0]):
        total = total + parts_ref[p]
    inverse_row = lax.rsqrt(total[0:1] * (1.0 / features) + EPSILON)
    slope_row = inverse_row * total[1:2] * (1.0 / features)
    decay_on = jnp.exp(-rate_row(facts_ref) * (rows_iota(BLOCK) + 1.0))
    over_block = power(facts_ref, float(BLOCK))
    carried = jnp.zeros((WIDTH, WIDTH), F32)
    gain_sum = jnp.zeros((1, WIDTH), F32)
    for b in reversed(range(q_ref.shape[0] // BLOCK)):
        rows = block_rows(b)
        lanes = slice(b * BLOCK, (b + 1) * BLOCK)
        inverse, slope = columns_of(inverse_row[:, lanes], slope_row[:, lanes])
        normed = attended_ref[rows] * inverse
        opening = jax.nn.sigmoid(gate_ref[rows].astype(F32))
        grad_open = cotangent_ref[rows].astype(F32) * opening
        gain_sum = gain_sum + jnp.sum(grad_open * normed, axis=0, keepdims=True)
        grad_norm = grad_open * gain_ref[...]
        grad = inverse * (grad_norm - normed * slope)
        grad_ref[rows] = beside(*split(grad))
        mixed_ref[rows] = (opening * gain_ref[...] * normed).astype(BF16)
        gate_grad_ref[rows] = (grad_norm * normed * (1.0 - opening)).astype(BF16)
        query_grad_ref[rows] = (
            inverse * (query_ref[0, rows] - inverse * slope * query_ref[1, rows])
        ).astype(BF16)
        piece = dot_split(q_ref[rows], decay_on * grad, 0)
        pieces_ref[b] = piece
        carried = (carried * over_block + piece) * kept(facts_ref, b)
    own_ref[...] = carried
    gain_part_ref[...] = gain_sum * (1.0 / math.sqrt(row_total))


def backward_kernel(
    facts_ref,
    q_ref,
    k_ref,
    v_ref,
    grad_ref,
    mixed_ref,
    gate_grad_ref,
    query_grad_ref,
    mixed_hbm,
    gate_grad_hbm,
    query_grad_hbm,
    key_part_ref,
    value_part_ref,
    sems,
):
    copies = [
        pltpu.make_async_copy(mixed_ref, mixed_hbm.at[0], sems.at[0]),
        pltpu.make_async_copy(gate_grad_ref, gate_grad_hbm.at[0], sems.at[1]),
        pltpu.make_async_copy(query_grad_ref, query_grad_hbm.at[0], sems.at[2]),
    ]
    for copy in copies:
        copy.start()
    weights = decay_matrix(facts_ref, 1)
    for b in range(q_ref.shape[0] // BLOCK):
        rows = block_rows(b)
        q, k, v, both = q_ref[rows], k_ref[rows], v_ref[rows], grad_ref[rows]
        high, low = split(dot(beside(v, v), both, 1, 1) * weights)
        key_part_ref[rows] = dot(high, q) + dot(low, q)
        high, low = split(dot(k, q, 1, 1) * weights)
        value_part_ref[rows] = halves(dot(high, both)) + dot(low, both[:, :WIDTH])
    for copy in copies:
        copy.wait()


def finish_kernel(
    tokens,
    place_ref,
    facts_ref,
    all_ref,
    other_ref,
    unbroken_ref,
    pieces_ref,
    k_ref,
    v_ref,
    key_part_ref,
    value_part_ref,
    key_grad_hbm,
    value_grad_hbm,
    gain_grad_ref,
    key_rows,
    value_rows,
    sems,
):
    copies = []
    place = place_ref[0]
    chip, core = place // 2, lax.rem(place, 2)
    over_slab = power(facts_ref, float(tokens))
    slabs = all_ref.shape[0]
    state = jnp.zeros((WIDTH, WIDTH), F32)
    for c in reversed(range(slabs // 2)):
        after = c > chip
        factor = unbroken_ref[2 * c : 2 * c + 1] * unbroken_ref[2 * c + 1 : 2 * c + 2]
        state = jnp.where(
            after, state * (factor * over_slab * over_slab) + chip_state(all_ref, c), state
        )
    partner = unbroken_ref[pl.ds(place - core + 1, 1)]
    state = jnp.where(core == 0, state * (partner * over_slab) + other_ref[...], state)
    gain = all_ref[0, HALF : HALF + 1]
    for s in range(1, slabs):
        gain = gain + all_ref[s, HALF : HALF + 1]
    gain_grad_ref[...] = gain
    decay_back = jnp.exp(-rate_row(facts_ref) * (float(BLOCK - 1) - rows_iota(BLOCK)))
    over_block = power(facts_ref, float(BLOCK))
    last = tokens // BLOCK - 1
    for b in reversed(range(last + 1)):
        rows = block_rows(b)
        if b < last:
            state = state * kept(facts_ref, b + 1)
        high, low = split(state)
        both = dot(k_ref[rows], beside(high, low))
        value_rows[rows] = (value_part_ref[rows] + decay_back * halves(both)).astype(BF16)
        both = dot(v_ref[rows], jnp.concatenate([high, low], axis=0), 1, 1)
        key_rows[rows] = (key_part_ref[rows] + decay_back * halves(both)).astype(BF16)
        for i, (source, target) in enumerate(
            ((key_rows, key_grad_hbm), (value_rows, value_grad_hbm))
        ):
            copy = pltpu.make_async_copy(
                source.at[rows], target.at[0, rows], sems.at[2 * b + i]
            )
            copy.start()
            copies.append(copy)
        state = state * over_block + pieces_ref[b]
    for copy in copies:
        copy.wait()


SMEM = pl.BlockSpec(memory_space=pltpu.SMEM)
VMEM = pl.BlockSpec(memory_space=pltpu.VMEM)
HBM = pl.BlockSpec(memory_space=pltpu.HBM)


def call(kernel, arrays, outs, flops=1 << 24, ins=None, out_specs=None, scratch=()):
    ins = ins or []
    moved = sum(math.prod(a.shape) * a.dtype.itemsize for a in (*arrays, *outs))
    return pl.pallas_call(
        kernel,
        out_shape=outs,
        in_specs=ins + [VMEM] * (len(arrays) - len(ins)),
        out_specs=out_specs or [VMEM] * len(outs),
        scratch_shapes=scratch,
        compiler_params=pltpu.CompilerParams(vmem_limit_bytes=LIMIT),
        cost_estimate=pl.CostEstimate(flops=flops, bytes_accessed=moved, transcendentals=0),
    )(*arrays)


def shape(*dims, dtype=F32):
    return jax.ShapeDtypeStruct(dims, dtype)


def bound(kernel, *fixed):
    def run(*refs):
        kernel(*fixed, *refs)

    return run


def body(queries, key_tokens, values, gate_logits, cotangent, decay_rates, norm_gain, block_starts):
    tokens = queries.shape[1]
    blocks = tokens // BLOCK
    slabs = lax.axis_size("ctx")
    outer, inner = lax.axis_size("dp"), lax.axis_size("pipe")
    features = float(WIDTH * outer * inner)
    place = lax.axis_index("ctx").astype(jnp.int32).reshape(1)
    partners = [(j, j ^ 1) for j in range(slabs)]
    whole = shape(1, tokens, WIDTH, dtype=BF16)
    like = shape(tokens, WIDTH, dtype=BF16)
    wide = shape(tokens, WIDTH)
    states = shape(blocks, WIDTH, WIDTH)
    two_wide = shape(2, tokens, WIDTH)
    dma = pltpu.SemaphoreType.DMA

    gate, cot = (a.reshape(tokens, WIDTH) for a in (gate_logits, cotangent))
    own, pairs, facts, keys, vals, quer, gain = call(
        closing_kernel,
        (
            decay_rates,
            *(
                pltpu.with_memory_space_constraint(a, pltpu.HBM)
                for a in (
                block_starts,
                key_tokens,
                values,
                queries,
                norm_gain,
                )
            ),
        ),
        [
            shape(WIDTH + 8, WIDTH),
            states,
            shape(8, BLOCK),
            like,
            like,
            like,
            shape(1, WIDTH),
        ],
        ins=[SMEM] + [HBM] * 5,
        scratch=[
            pltpu.SMEM((1, blocks), jnp.int32),
            dma((3 + 2 * blocks,)),
        ],
    )
    other = lax.ppermute(own, "ctx", partners)
    (local,) = call(local_kernel, (facts, quer, keys, vals), [wide], flops=1 << 28)
    (half,) = call(
        bound(forward_half_kernel, tokens),
        (place, facts, own, other),
        [shape(HALF + 8, WIDTH)],
        ins=[SMEM],
    )
    everyone = lax.all_gather(half, "ctx")
    attended, states_in, sums, unbroken = call(
        bound(attended_kernel, tokens),
        (place, facts, everyone, other, pairs, quer, local, gate, cot, gain),
        [wide, states, shape(inner, 2, tokens), shape(slabs, WIDTH)],
        ins=[SMEM],
    )
    sums = lax.all_to_all(sums, "pipe", 0, 0, tiled=True)
    (sums,) = call(spread_kernel, (sums,), [shape(outer, 2, tokens)])
    sums = lax.all_to_all(sums, "dp", 0, 0, tiled=True)
    (query_parts,) = call(
        beforehand_kernel,
        (facts, keys, vals, gate, cot, gain, attended, states_in),
        [shape(2, tokens, WIDTH)],
        flops=1 << 30,
    )
    back, gain_part, grad, pieces, mixed, gate_part, query_part = call(
        bound(grad_kernel, features, tokens * slabs),
        (facts, sums, attended, quer, gate, cot, gain, query_parts),
        [
            shape(WIDTH, WIDTH),
            shape(1, WIDTH),
            shape(tokens, 2 * WIDTH, dtype=BF16),
            states,
            like,
            like,
            like,
        ],
    )
    back_other = lax.ppermute(back, "ctx", partners)
    mixed_out, gate_grad, query_grad, key_part, value_part = call(
        backward_kernel,
        (facts, quer, keys, vals, grad, mixed, gate_part, query_part),
        [whole, whole, whole, wide, wide],
        out_specs=[HBM] * 3 + [VMEM] * 2,
        scratch=[dma((3,))],
        flops=1 << 30,
    )
    (back_half,) = call(
        bound(backward_half_kernel, tokens),
        (place, facts, back, back_other, gain_part, unbroken),
        [shape(HALF + 8, WIDTH)],
        ins=[SMEM],
    )
    back_everyone = lax.all_gather(back_half, "ctx")
    key_grad, value_grad, gain_grad = call(
        bound(finish_kernel, tokens),
        (
            place,
            facts,
            back_everyone,
            back_other,
            unbroken,
            pieces,
            keys,
            vals,
            key_part,
            value_part,
        ),
        [whole, whole, shape(1, WIDTH)],
        ins=[SMEM],
        out_specs=[HBM] * 2 + [VMEM],
        scratch=[
            pltpu.VMEM((tokens, WIDTH), BF16),
            pltpu.VMEM((tokens, WIDTH), BF16),
            dma((2 * blocks,)),
        ],
    )
    return (mixed_out, query_grad, key_grad, value_grad, gate_grad, gain_grad)


def solution(mesh):
    wide = P(None, "ctx", ("dp", "pipe"))
    heads = P(("dp", "pipe"))
    gain = P(("dp", "pipe"), None)
    return jax.shard_map(
        body,
        mesh=mesh,
        in_specs=(wide, wide, wide, wide, wide, heads, gain, P(None, "ctx")),
        out_specs=(wide, wide, wide, wide, wide, gain),
        check_vma=False,
    )
```

```python
import math

import jax
import jax.numpy as jnp
from jax import lax
from jax.experimental import pallas as pl
from jax.experimental.pallas import tpu as pltpu
from jax.sharding import PartitionSpec as P

BLOCK = 256
EPSILON = 1e-06
F32 = jnp.float32
BF16 = jnp.bfloat16
WIDTH = 128
HALF = 64
LIMIT = 12 << 20


def split(x):
    high = x.astype(BF16)
    return high, (x - high.astype(F32)).astype(BF16)


def dot(a, b, da=1, db=0):
    return lax.dot_general(a, b, (((da,), (db,)), ((), ())), preferred_element_type=F32)


def dot_split(a, x, da=1):
    high, low = split(x)
    both = dot(a, jnp.concatenate([high, low], axis=1), da, 0)
    n = x.shape[1]
    return both[:, :n] + both[:, n:]


def rows_iota(rows, columns=WIDTH):
    return lax.broadcasted_iota(jnp.int32, (rows, columns), 0).astype(F32)


def power(facts_ref, tokens):
    return jnp.exp(-rate_row(facts_ref) * tokens)


def rate_row(facts_ref):
    return facts_ref[0:1, :WIDTH]


def kept(facts_ref, b):
    return facts_ref[b + 1 : b + 2, :WIDTH]


def block_rows(b):
    return pl.ds(b * BLOCK, BLOCK)


def decay_matrix(facts_ref, at_axis=0):
    at = lax.broadcasted_iota(jnp.int32, (BLOCK, BLOCK), at_axis)
    of = lax.broadcasted_iota(jnp.int32, (BLOCK, BLOCK), 1 - at_axis)
    distance = (at - of).astype(F32)
    return jnp.where(
        distance >= 0, jnp.exp(-facts_ref[0:1] * jnp.maximum(distance, 0.0)), 0.0
    )


def halves(both):
    return both[:, :WIDTH] + both[:, WIDTH:]


def beside(a, b):
    return jnp.concatenate([a, b], axis=1)


def closing_kernel(
    rate_ref,
    flags_hbm,
    k_hbm,
    v_hbm,
    q_hbm,
    gain_hbm,
    own_ref,
    pairs_ref,
    facts_ref,
    k_ref,
    v_ref,
    q_ref,
    gain_ref,
    flags_smem,
    sems,
):
    blocks = k_ref.shape[0] // BLOCK
    flags_copy = pltpu.make_async_copy(flags_hbm, flags_smem, sems.at[0])
    flags_copy.start()
    parts = []
    for b in range(blocks):
        rows = block_rows(b)
        parts.append(
            [
                pltpu.make_async_copy(k_hbm.at[0, rows], k_ref.at[rows], sems.at[1 + 2 * b]),
                pltpu.make_async_copy(v_hbm.at[0, rows], v_ref.at[rows], sems.at[2 + 2 * b]),
            ]
        )
        for copy in parts[b]:
            copy.start()
    at = 1 + 2 * blocks
    rest = [
        pltpu.make_async_copy(q_hbm.at[0], q_ref, sems.at[at]),
        pltpu.make_async_copy(gain_hbm, gain_ref, sems.at[at + 1]),
    ]
    for copy in rest:
        copy.start()
    facts_ref[0:1] = jnp.full((1, BLOCK), rate_ref[0], F32)
    rate = jnp.full((1, WIDTH), rate_ref[0], F32)
    decay_out = jnp.exp(-rate * (float(BLOCK) - rows_iota(BLOCK)))
    over_block = jnp.exp(-rate * float(BLOCK))
    for b in range(blocks):
        for copy in parts[b]:
            copy.wait()
        rows = block_rows(b)
        pairs_ref[b] = dot_split(k_ref[rows], decay_out * v_ref[rows].astype(F32), 0)
    flags_copy.wait()
    unbroken = 1.0
    carried = jnp.zeros((WIDTH, WIDTH), F32)
    for b in range(blocks):
        keep = 1.0 - flags_smem[0, b].astype(F32)
        unbroken = unbroken * keep
        facts_ref[b + 1 : b + 2] = jnp.full((1, BLOCK), keep, F32)
        carried = carried * (over_block * keep) + pairs_ref[b]
    own_ref[:WIDTH] = carried
    own_ref[WIDTH:] = jnp.full((8, WIDTH), unbroken, F32)
    for copy in rest:
        copy.wait()


def local_kernel(facts_ref, q_ref, k_ref, v_ref, out_ref):
    weights = decay_matrix(facts_ref)
    blocks = q_ref.shape[0] // BLOCK
    ahead = None
    for b in range(blocks + 1):
        coming = None
        if b < blocks:
            rows = block_rows(b)
            scores = dot(q_ref[rows], k_ref[rows], 1, 1)
        if ahead is not None:
            before = block_rows(b - 1)
            v = v_ref[before]
            out_ref[before] = dot(ahead[0], v) + dot(ahead[1], v)
        if b < blocks:
            coming = split(scores * weights)
        ahead = coming


def forward_half_kernel(tokens, place_ref, facts_ref, own_ref, other_ref, out_ref):
    second = lax.rem(place_ref[0], 2) == 1
    over_slab = power(facts_ref, float(tokens))
    own, other = own_ref[:WIDTH], other_ref[:WIDTH]
    early = jnp.where(second, other, own)
    late = jnp.where(second, own, other)
    late_kept = jnp.where(second, own_ref[WIDTH : WIDTH + 1], other_ref[WIDTH : WIDTH + 1])
    chip = early * (late_kept * over_slab) + late
    out_ref[:HALF] = jnp.where(second, chip[HALF:], chip[:HALF])
    out_ref[HALF:] = own_ref[WIDTH:]


def backward_half_kernel(
    tokens, place_ref, facts_ref, own_ref, other_ref, gain_ref, unbroken_ref, out_ref
):
    place = place_ref[0]
    second = lax.rem(place, 2) == 1
    over_slab = power(facts_ref, float(tokens))
    own, other = own_ref[...], other_ref[...]
    early = jnp.where(second, other, own)
    late = jnp.where(second, own, other)
    early_kept = unbroken_ref[pl.ds(place - lax.rem(place, 2), 1)]
    chip = late * (early_kept * over_slab) + early
    out_ref[:HALF] = jnp.where(second, chip[HALF:], chip[:HALF])
    out_ref[HALF:] = jnp.broadcast_to(gain_ref[...], (8, WIDTH))


def chip_state(all_ref, c):
    return jnp.concatenate([all_ref[2 * c, :HALF], all_ref[2 * c + 1, :HALF]], axis=0)


def attended_kernel(
    tokens,
    place_ref,
    facts_ref,
    all_ref,
    other_ref,
    pairs_ref,
    q_ref,
    local_ref,
    gate_ref,
    cotangent_ref,
    gain_ref,
    attended_ref,
    states_ref,
    sums_ref,
    unbroken_ref,
):
    place = place_ref[0]
    chip, core = place // 2, lax.rem(place, 2)
    over_slab = power(facts_ref, float(tokens))
    slabs = all_ref.shape[0]
    state = jnp.zeros((WIDTH, WIDTH), F32)
    for c in range(slabs // 2):
        before = c < chip
        factor = all_ref[2 * c, HALF : HALF + 1] * all_ref[2 * c + 1, HALF : HALF + 1]
        state = jnp.where(
            before, state * (factor * over_slab * over_slab) + chip_state(all_ref, c), state
        )
    state = jnp.where(
        core == 1,
        state * (other_ref[WIDTH : WIDTH + 1] * over_slab) + other_ref[:WIDTH],
        state,
    )
    for s in range(slabs):
        unbroken_ref[s : s + 1] = all_ref[s, HALF : HALF + 1]
    decay_in = jnp.exp(-rate_row(facts_ref) * rows_iota(BLOCK))
    over_block = power(facts_ref, float(BLOCK))
    ones = jnp.ones((8, 2 * WIDTH), BF16)
    first = lax.broadcasted_iota(jnp.int32, (8, BLOCK), 0) == 0
    blocks = tokens // BLOCK
    for b in range(blocks):
        state = state * kept(facts_ref, b)
        states_ref[b] = state
        state = state * over_block + pairs_ref[b]

    def across(b):
        high, low = split(states_ref[b])
        return dot(q_ref[block_rows(b)], beside(high, low))

    ahead, behind = across(0), None
    for b in range(blocks + 1):
        coming = across(b + 1) if b + 1 < blocks else None
        if b < blocks:
            rows = block_rows(b)
            attended = local_ref[rows] + decay_in * halves(ahead)
            attended_ref[rows] = attended
            opening = jax.nn.sigmoid(gate_ref[rows].astype(F32))
            grad_norm = cotangent_ref[rows].astype(F32) * opening * gain_ref[...]
            squares = dot(ones, beside(*split(attended * attended)), 1, 1)
            crosses = dot(ones, beside(*split(grad_norm * attended)), 1, 1)
        if behind is not None:
            both = jnp.where(first, *behind)[:2]
            for p in range(sums_ref.shape[0]):
                sums_ref[p, :, (b - 1) * BLOCK : b * BLOCK] = both
        ahead, behind = coming, (squares, crosses)


def spread_kernel(parts_ref, out_ref):
    total = parts_ref[0]
    for p in range(1, parts_ref.shape[0]):
        total = total + parts_ref[p]
    for p in range(out_ref.shape[0]):
        out_ref[p] = total


def beforehand_kernel(
    facts_ref,
    k_ref,
    v_ref,
    gate_ref,
    cotangent_ref,
    gain_ref,
    attended_ref,
    states_ref,
    query_ref,
):
    weights = decay_matrix(facts_ref)
    decay_in = jnp.exp(-rate_row(facts_ref) * rows_iota(BLOCK))
    for b in range(k_ref.shape[0] // BLOCK):
        rows = block_rows(b)
        k, v = k_ref[rows], v_ref[rows]
        opening = jax.nn.sigmoid(gate_ref[rows].astype(F32))
        grad_norm = cotangent_ref[rows].astype(F32) * opening * gain_ref[...]
        twice = beside(v, v)
        state_high, state_low = split(states_ref[b])
        state_twice = beside(state_high, state_high)
        for i, left in enumerate((grad_norm, attended_ref[rows])):
            high, low = split(left)
            both = beside(high, low)
            across = dot(both, state_twice, 1, 1) + dot(high, state_low, 1, 1)
            high, low = split(dot(both, twice, 1, 1) * weights)
            query_ref[i, rows] = dot(high, k) + dot(low, k) + decay_in * across


def thirds(row):
    high = row.astype(BF16).astype(F32)
    rest = row - high
    middle = rest.astype(BF16).astype(F32)
    return high, middle, rest - middle


def columns_of(first, second):
    pieces = thirds(first) + thirds(second)
    n = first.shape[1]
    at = lax.broadcasted_iota(jnp.int32, (16, n), 0)
    stacked = jnp.zeros((16, n), F32)
    for i, piece in enumerate(pieces):
        stacked = jnp.where(at == i, piece, stacked)
    row = lax.broadcasted_iota(jnp.int32, (16, 2 * WIDTH), 0)
    column = lax.broadcasted_iota(jnp.int32, (16, 2 * WIDTH), 1)
    chosen = jnp.where((row >= 3) == (column >= WIDTH), 1.0, 0.0).astype(BF16)
    both = dot(stacked.astype(BF16), chosen, 0, 0)
    return both[:, :WIDTH], both[:, WIDTH:]


def grad_kernel(
    features,
    row_total,
    facts_ref,
    parts_ref,
    attended_ref,
    q_ref,
    gate_ref,
    cotangent_ref,
    gain_ref,
    query_ref,
    own_ref,
    gain_part_ref,
    grad_ref,
    pieces_ref,
    mixed_ref,
    gate_grad_ref,
    query_grad_ref,
):
    total = parts_ref[0]
    for p in range(1, parts_ref.shape[0]):
        total = total + parts_ref[p]
    inverse_row = lax.rsqrt(total[0:1] * (1.0 / features) + EPSILON)
    slope_row = inverse_row * total[1:2] * (1.0 / features)
    decay_on = jnp.exp(-rate_row(facts_ref) * (rows_iota(BLOCK) + 1.0))
    over_block = power(facts_ref, float(BLOCK))
    carried = jnp.zeros((WIDTH, WIDTH), F32)
    gain_sum = jnp.zeros((1, WIDTH), F32)
    blocks = q_ref.shape[0] // BLOCK

    def columns(b):
        lanes = slice(b * BLOCK, (b + 1) * BLOCK)
        return columns_of(inverse_row[:, lanes], slope_row[:, lanes])

    ahead, behind = columns(blocks - 1), None
    for b in reversed(range(-1, blocks)):
        coming = columns(b - 1) if b > 0 else None
        piece = None
        if b >= 0:
            rows = block_rows(b)
            inverse, slope = ahead
            normed = attended_ref[rows] * inverse
            opening = jax.nn.sigmoid(gate_ref[rows].astype(F32))
            grad_open = cotangent_ref[rows].astype(F32) * opening
            gain_sum = gain_sum + jnp.sum(grad_open * normed, axis=0, keepdims=True)
            grad_norm = grad_open * gain_ref[...]
            grad = inverse * (grad_norm - normed * slope)
            piece = dot_split(q_ref[rows], decay_on * grad, 0)
            grad_ref[rows] = beside(*split(grad))
            mixed_ref[rows] = (opening * gain_ref[...] * normed).astype(BF16)
            gate_grad_ref[rows] = (grad_norm * normed * (1.0 - opening)).astype(BF16)
            query_grad_ref[rows] = (
                inverse * (query_ref[0, rows] - inverse * slope * query_ref[1, rows])
            ).astype(BF16)
        if behind is not None:
            pieces_ref[b + 1] = behind
            carried = (carried * over_block + behind) * kept(facts_ref, b + 1)
        ahead, behind = coming, piece
    own_ref[...] = carried
    gain_part_ref[...] = gain_sum * (1.0 / math.sqrt(row_total))


def backward_kernel(
    facts_ref,
    q_ref,
    k_ref,
    v_ref,
    grad_ref,
    mixed_ref,
    gate_grad_ref,
    query_grad_ref,
    mixed_hbm,
    gate_grad_hbm,
    query_grad_hbm,
    key_part_ref,
    value_part_ref,
    sems,
):
    copies = [
        pltpu.make_async_copy(mixed_ref, mixed_hbm.at[0], sems.at[0]),
        pltpu.make_async_copy(gate_grad_ref, gate_grad_hbm.at[0], sems.at[1]),
        pltpu.make_async_copy(query_grad_ref, query_grad_hbm.at[0], sems.at[2]),
    ]
    for copy in copies:
        copy.start()
    weights = decay_matrix(facts_ref, 1)
    blocks = q_ref.shape[0] // BLOCK
    ahead = None
    for b in range(blocks + 1):
        coming = None
        if b < blocks:
            rows = block_rows(b)
            v = v_ref[rows]
            slopes = dot(beside(v, v), grad_ref[rows], 1, 1)
            scores = dot(k_ref[rows], q_ref[rows], 1, 1)
        if ahead is not None:
            (slopes_high, slopes_low), (scores_high, scores_low) = ahead
            before = block_rows(b - 1)
            q, both = q_ref[before], grad_ref[before]
            key_part_ref[before] = dot(slopes_high, q) + dot(slopes_low, q)
            value_part_ref[before] = halves(dot(scores_high, both)) + dot(
                scores_low, both[:, :WIDTH]
            )
        if b < blocks:
            coming = split(slopes * weights), split(scores * weights)
        ahead = coming
    for copy in copies:
        copy.wait()


def finish_kernel(
    tokens,
    place_ref,
    facts_ref,
    all_ref,
    other_ref,
    unbroken_ref,
    pieces_ref,
    k_ref,
    v_ref,
    key_part_ref,
    value_part_ref,
    key_grad_hbm,
    value_grad_hbm,
    gain_grad_ref,
    key_rows,
    value_rows,
    sems,
):
    copies = []
    place = place_ref[0]
    chip, core = place // 2, lax.rem(place, 2)
    over_slab = power(facts_ref, float(tokens))
    slabs = all_ref.shape[0]
    state = jnp.zeros((WIDTH, WIDTH), F32)
    for c in reversed(range(slabs // 2)):
        after = c > chip
        factor = unbroken_ref[2 * c : 2 * c + 1] * unbroken_ref[2 * c + 1 : 2 * c + 2]
        state = jnp.where(
            after, state * (factor * over_slab * over_slab) + chip_state(all_ref, c), state
        )
    partner = unbroken_ref[pl.ds(place - core + 1, 1)]
    state = jnp.where(core == 0, state * (partner * over_slab) + other_ref[...], state)
    gain = all_ref[0, HALF : HALF + 1]
    for s in range(1, slabs):
        gain = gain + all_ref[s, HALF : HALF + 1]
    gain_grad_ref[...] = gain
    decay_back = jnp.exp(-rate_row(facts_ref) * (float(BLOCK - 1) - rows_iota(BLOCK)))
    over_block = power(facts_ref, float(BLOCK))
    last = tokens // BLOCK - 1
    for b in reversed(range(last + 1)):
        rows = block_rows(b)
        if b < last:
            state = state * kept(facts_ref, b + 1)
        high, low = split(state)
        both = dot(k_ref[rows], beside(high, low))
        value_rows[rows] = (value_part_ref[rows] + decay_back * halves(both)).astype(BF16)
        both = dot(v_ref[rows], jnp.concatenate([high, low], axis=0), 1, 1)
        key_rows[rows] = (key_part_ref[rows] + decay_back * halves(both)).astype(BF16)
        for i, (source, target) in enumerate(
            ((key_rows, key_grad_hbm), (value_rows, value_grad_hbm))
        ):
            copy = pltpu.make_async_copy(
                source.at[rows], target.at[0, rows], sems.at[2 * b + i]
            )
            copy.start()
            copies.append(copy)
        state = state * over_block + pieces_ref[b]
    for copy in copies:
        copy.wait()


SMEM = pl.BlockSpec(memory_space=pltpu.SMEM)
VMEM = pl.BlockSpec(memory_space=pltpu.VMEM)
HBM = pl.BlockSpec(memory_space=pltpu.HBM)


def call(kernel, arrays, outs, flops=1 << 24, ins=None, out_specs=None, scratch=()):
    ins = ins or []
    moved = sum(math.prod(a.shape) * a.dtype.itemsize for a in (*arrays, *outs))
    return pl.pallas_call(
        kernel,
        out_shape=outs,
        in_specs=ins + [VMEM] * (len(arrays) - len(ins)),
        out_specs=out_specs or [VMEM] * len(outs),
        scratch_shapes=scratch,
        compiler_params=pltpu.CompilerParams(vmem_limit_bytes=LIMIT),
        cost_estimate=pl.CostEstimate(flops=flops, bytes_accessed=moved, transcendentals=0),
    )(*arrays)


def shape(*dims, dtype=F32):
    return jax.ShapeDtypeStruct(dims, dtype)


def bound(kernel, *fixed):
    def run(*refs):
        kernel(*fixed, *refs)

    return run


def body(queries, key_tokens, values, gate_logits, cotangent, decay_rates, norm_gain, block_starts):
    tokens = queries.shape[1]
    blocks = tokens // BLOCK
    slabs = lax.axis_size("ctx")
    outer, inner = lax.axis_size("dp"), lax.axis_size("pipe")
    features = float(WIDTH * outer * inner)
    place = lax.axis_index("ctx").astype(jnp.int32).reshape(1)
    partners = [(j, j ^ 1) for j in range(slabs)]
    whole = shape(1, tokens, WIDTH, dtype=BF16)
    like = shape(tokens, WIDTH, dtype=BF16)
    wide = shape(tokens, WIDTH)
    states = shape(blocks, WIDTH, WIDTH)
    two_wide = shape(2, tokens, WIDTH)
    dma = pltpu.SemaphoreType.DMA

    gate, cot = (a.reshape(tokens, WIDTH) for a in (gate_logits, cotangent))
    own, pairs, facts, keys, vals, quer, gain = call(
        closing_kernel,
        (
            decay_rates,
            *(
                pltpu.with_memory_space_constraint(a, pltpu.HBM)
                for a in (
                block_starts,
                key_tokens,
                values,
                queries,
                norm_gain,
                )
            ),
        ),
        [
            shape(WIDTH + 8, WIDTH),
            states,
            shape(8, BLOCK),
            like,
            like,
            like,
            shape(1, WIDTH),
        ],
        ins=[SMEM] + [HBM] * 5,
        scratch=[
            pltpu.SMEM((1, blocks), jnp.int32),
            dma((3 + 2 * blocks,)),
        ],
    )
    other = lax.ppermute(own, "ctx", partners)
    (local,) = call(local_kernel, (facts, quer, keys, vals), [wide], flops=1 << 28)
    (half,) = call(
        bound(forward_half_kernel, tokens),
        (place, facts, own, other),
        [shape(HALF + 8, WIDTH)],
        ins=[SMEM],
    )
    everyone = lax.all_gather(half, "ctx")
    attended, states_in, sums, unbroken = call(
        bound(attended_kernel, tokens),
        (place, facts, everyone, other, pairs, quer, local, gate, cot, gain),
        [wide, states, shape(inner, 2, tokens), shape(slabs, WIDTH)],
        ins=[SMEM],
    )
    sums = lax.all_to_all(sums, "pipe", 0, 0, tiled=True)
    (sums,) = call(spread_kernel, (sums,), [shape(outer, 2, tokens)])
    sums = lax.all_to_all(sums, "dp", 0, 0, tiled=True)
    (query_parts,) = call(
        beforehand_kernel,
        (facts, keys, vals, gate, cot, gain, attended, states_in),
        [shape(2, tokens, WIDTH)],
        flops=1 << 30,
    )
    back, gain_part, grad, pieces, mixed, gate_part, query_part = call(
        bound(grad_kernel, features, tokens * slabs),
        (facts, sums, attended, quer, gate, cot, gain, query_parts),
        [
            shape(WIDTH, WIDTH),
            shape(1, WIDTH),
            shape(tokens, 2 * WIDTH, dtype=BF16),
            states,
            like,
            like,
            like,
        ],
    )
    back_other = lax.ppermute(back, "ctx", partners)
    mixed_out, gate_grad, query_grad, key_part, value_part = call(
        backward_kernel,
        (facts, quer, keys, vals, grad, mixed, gate_part, query_part),
        [whole, whole, whole, wide, wide],
        out_specs=[HBM] * 3 + [VMEM] * 2,
        scratch=[dma((3,))],
        flops=1 << 30,
    )
    (back_half,) = call(
        bound(backward_half_kernel, tokens),
        (place, facts, back, back_other, gain_part, unbroken),
        [shape(HALF + 8, WIDTH)],
        ins=[SMEM],
    )
    back_everyone = lax.all_gather(back_half, "ctx")
    key_grad, value_grad, gain_grad = call(
        bound(finish_kernel, tokens),
        (
            place,
            facts,
            back_everyone,
            back_other,
            unbroken,
            pieces,
            keys,
            vals,
            key_part,
            value_part,
        ),
        [whole, whole, shape(1, WIDTH)],
        ins=[SMEM],
        out_specs=[HBM] * 2 + [VMEM],
        scratch=[
            pltpu.VMEM((tokens, WIDTH), BF16),
            pltpu.VMEM((tokens, WIDTH), BF16),
            dma((2 * blocks,)),
        ],
    )
    return (mixed_out, query_grad, key_grad, value_grad, gate_grad, gain_grad)


def solution(mesh):
    wide = P(None, "ctx", ("dp", "pipe"))
    heads = P(("dp", "pipe"))
    gain = P(("dp", "pipe"), None)
    return jax.shard_map(
        body,
        mesh=mesh,
        in_specs=(wide, wide, wide, wide, wide, heads, gain, P(None, "ctx")),
        out_specs=(wide, wide, wide, wide, wide, gain),
        check_vma=False,
    )
```

```python
import math

import jax
import jax.numpy as jnp
from jax import lax
from jax.experimental import pallas as pl
from jax.experimental.pallas import tpu as pltpu
from jax.sharding import PartitionSpec as P

BLOCK = 256
EPSILON = 1e-06
F32 = jnp.float32
BF16 = jnp.bfloat16
WIDTH = 128
HALF = 64
LIMIT = 12 << 20


def split(x):
    high = x.astype(BF16)
    return high, (x - high.astype(F32)).astype(BF16)


def dot(a, b, da=1, db=0):
    return lax.dot_general(a, b, (((da,), (db,)), ((), ())), preferred_element_type=F32)


def dot_split(a, x, da=1):
    high, low = split(x)
    both = dot(a, jnp.concatenate([high, low], axis=1), da, 0)
    n = x.shape[1]
    return both[:, :n] + both[:, n:]


def rows_iota(rows, columns=WIDTH):
    return lax.broadcasted_iota(jnp.int32, (rows, columns), 0).astype(F32)


def power(facts_ref, tokens):
    return jnp.exp(-rate_row(facts_ref) * tokens)


def rate_row(facts_ref):
    return facts_ref[0:1, :WIDTH]


def kept(facts_ref, b):
    return facts_ref[b + 1 : b + 2, :WIDTH]


def block_rows(b):
    return pl.ds(b * BLOCK, BLOCK)


def decay_matrix(facts_ref, at_axis=0):
    at = lax.broadcasted_iota(jnp.int32, (BLOCK, BLOCK), at_axis)
    of = lax.broadcasted_iota(jnp.int32, (BLOCK, BLOCK), 1 - at_axis)
    distance = (at - of).astype(F32)
    return jnp.where(
        distance >= 0, jnp.exp(-facts_ref[0:1] * jnp.maximum(distance, 0.0)), 0.0
    )


def halves(both):
    return both[:, :WIDTH] + both[:, WIDTH:]


def beside(a, b):
    return jnp.concatenate([a, b], axis=1)


def closing_kernel(
    rate_ref,
    flags_hbm,
    k_hbm,
    v_hbm,
    q_hbm,
    gain_hbm,
    own_ref,
    pairs_ref,
    facts_ref,
    k_ref,
    v_ref,
    q_ref,
    gain_ref,
    flags_smem,
    sems,
):
    blocks = k_ref.shape[0] // BLOCK
    flags_copy = pltpu.make_async_copy(flags_hbm, flags_smem, sems.at[0])
    flags_copy.start()
    parts = [
        pltpu.make_async_copy(k_hbm.at[0], k_ref, sems.at[1]),
        pltpu.make_async_copy(v_hbm.at[0], v_ref, sems.at[2]),
    ]
    for copy in parts:
        copy.start()
    rest = [
        pltpu.make_async_copy(q_hbm.at[0], q_ref, sems.at[3]),
        pltpu.make_async_copy(gain_hbm, gain_ref, sems.at[4]),
    ]
    for copy in rest:
        copy.start()
    facts_ref[0:1] = jnp.full((1, BLOCK), rate_ref[0], F32)
    rate = jnp.full((1, WIDTH), rate_ref[0], F32)
    decay_out = jnp.exp(-rate * (float(BLOCK) - rows_iota(BLOCK)))
    over_block = jnp.exp(-rate * float(BLOCK))
    flags_copy.wait()
    for copy in parts:
        copy.wait()
    pieces = []
    for b in range(blocks):
        rows = block_rows(b)
        pieces.append(dot_split(k_ref[rows], decay_out * v_ref[rows].astype(F32), 0))
    unbroken = 1.0
    carried = jnp.zeros((WIDTH, WIDTH), F32)
    for b in range(blocks):
        keep = 1.0 - flags_smem[0, b].astype(F32)
        unbroken = unbroken * keep
        facts_ref[b + 1 : b + 2] = jnp.full((1, BLOCK), keep, F32)
        pairs_ref[b] = pieces[b]
        carried = carried * (over_block * keep) + pieces[b]
    own_ref[:WIDTH] = carried
    own_ref[WIDTH:] = jnp.full((8, WIDTH), unbroken, F32)
    for copy in rest:
        copy.wait()


def local_kernel(facts_ref, q_ref, k_ref, v_ref, out_ref):
    weights = decay_matrix(facts_ref)
    blocks = q_ref.shape[0] // BLOCK
    ahead = None
    for b in range(blocks + 1):
        coming = None
        if b < blocks:
            rows = block_rows(b)
            scores = dot(q_ref[rows], k_ref[rows], 1, 1)
        if ahead is not None:
            before = block_rows(b - 1)
            v = v_ref[before]
            out_ref[before] = dot(ahead[0], v) + dot(ahead[1], v)
        if b < blocks:
            coming = split(scores * weights)
        ahead = coming


def forward_half_kernel(tokens, place_ref, facts_ref, own_ref, other_ref, out_ref):
    second = lax.rem(place_ref[0], 2) == 1
    over_slab = power(facts_ref, float(tokens))
    own, other = own_ref[:WIDTH], other_ref[:WIDTH]
    early = jnp.where(second, other, own)
    late = jnp.where(second, own, other)
    late_kept = jnp.where(second, own_ref[WIDTH : WIDTH + 1], other_ref[WIDTH : WIDTH + 1])
    chip = early * (late_kept * over_slab) + late
    out_ref[:HALF] = jnp.where(second, chip[HALF:], chip[:HALF])
    out_ref[HALF:] = own_ref[WIDTH:]


def backward_half_kernel(
    tokens, place_ref, facts_ref, own_ref, other_ref, gain_ref, unbroken_ref, out_ref
):
    place = place_ref[0]
    second = lax.rem(place, 2) == 1
    over_slab = power(facts_ref, float(tokens))
    own, other = own_ref[...], other_ref[...]
    early = jnp.where(second, other, own)
    late = jnp.where(second, own, other)
    early_kept = unbroken_ref[pl.ds(place - lax.rem(place, 2), 1)]
    chip = late * (early_kept * over_slab) + early
    out_ref[:HALF] = jnp.where(second, chip[HALF:], chip[:HALF])
    out_ref[HALF:] = jnp.broadcast_to(gain_ref[...], (8, WIDTH))


def chip_state(all_ref, c):
    return jnp.concatenate([all_ref[2 * c, :HALF], all_ref[2 * c + 1, :HALF]], axis=0)


def attended_kernel(
    tokens,
    place_ref,
    facts_ref,
    all_ref,
    other_ref,
    pairs_ref,
    q_ref,
    local_ref,
    gate_ref,
    cotangent_ref,
    gain_ref,
    attended_ref,
    states_ref,
    sums_ref,
    unbroken_ref,
):
    place = place_ref[0]
    chip, core = place // 2, lax.rem(place, 2)
    over_slab = power(facts_ref, float(tokens))
    slabs = all_ref.shape[0]
    state = jnp.zeros((WIDTH, WIDTH), F32)
    along = jnp.ones((1, WIDTH), F32)
    for c in reversed(range(slabs // 2)):
        before = c < chip
        factor = all_ref[2 * c, HALF : HALF + 1] * all_ref[2 * c + 1, HALF : HALF + 1]
        state = state + chip_state(all_ref, c) * jnp.where(before, along, 0.0)
        along = jnp.where(before, along * (factor * over_slab * over_slab), along)
    state = jnp.where(
        core == 1,
        state * (other_ref[WIDTH : WIDTH + 1] * over_slab) + other_ref[:WIDTH],
        state,
    )
    for s in range(slabs):
        unbroken_ref[s : s + 1] = all_ref[s, HALF : HALF + 1]
    decay_in = jnp.exp(-rate_row(facts_ref) * rows_iota(BLOCK))
    over_block = power(facts_ref, float(BLOCK))
    ones = jnp.ones((8, 2 * WIDTH), BF16)
    first = lax.broadcasted_iota(jnp.int32, (8, BLOCK), 0) == 0
    blocks = tokens // BLOCK
    for b in range(blocks):
        state = state * kept(facts_ref, b)
        states_ref[b] = state
        state = state * over_block + pairs_ref[b]

    def across(b):
        high, low = split(states_ref[b])
        q = q_ref[block_rows(b)]
        return dot(beside(q, q), jnp.concatenate([high, low], axis=0))

    ahead, behind = across(0), None
    for b in range(blocks + 1):
        coming = across(b + 1) if b + 1 < blocks else None
        if b < blocks:
            rows = block_rows(b)
            attended = local_ref[rows] + decay_in * ahead
            attended_ref[rows] = attended
            opening = jax.nn.sigmoid(gate_ref[rows].astype(F32))
            grad_norm = cotangent_ref[rows].astype(F32) * opening * gain_ref[...]
            squares = dot(ones, beside(*split(attended * attended)), 1, 1)
            crosses = dot(ones, beside(*split(grad_norm * attended)), 1, 1)
        if behind is not None:
            both = jnp.where(first, *behind)[:2]
            for p in range(sums_ref.shape[0]):
                sums_ref[p, :, (b - 1) * BLOCK : b * BLOCK] = both
        ahead, behind = coming, (squares, crosses)


def spread_kernel(parts_ref, out_ref):
    total = parts_ref[0]
    for p in range(1, parts_ref.shape[0]):
        total = total + parts_ref[p]
    for p in range(out_ref.shape[0]):
        out_ref[p] = total


def beforehand_kernel(
    facts_ref,
    k_ref,
    v_ref,
    gate_ref,
    cotangent_ref,
    gain_ref,
    attended_ref,
    states_ref,
    query_ref,
):
    weights = decay_matrix(facts_ref)
    decay_in = jnp.exp(-rate_row(facts_ref) * rows_iota(BLOCK))
    for b in range(k_ref.shape[0] // BLOCK):
        rows = block_rows(b)
        k, v = k_ref[rows], v_ref[rows]
        opening = jax.nn.sigmoid(gate_ref[rows].astype(F32))
        grad_norm = cotangent_ref[rows].astype(F32) * opening * gain_ref[...]
        twice = beside(v, v)
        state_high, state_low = split(states_ref[b])
        state_twice = beside(state_high, state_high)
        for i, left in enumerate((grad_norm, attended_ref[rows])):
            high, low = split(left)
            both = beside(high, low)
            across = dot(both, state_twice, 1, 1) + dot(high, state_low, 1, 1)
            high, low = split(dot(both, twice, 1, 1) * weights)
            query_ref[i, rows] = dot(high, k) + dot(low, k) + decay_in * across


def thirds(row):
    high = row.astype(BF16).astype(F32)
    rest = row - high
    middle = rest.astype(BF16).astype(F32)
    return high, middle, rest - middle


def columns_of(first, second):
    pieces = thirds(first) + thirds(second)
    n = first.shape[1]
    at = lax.broadcasted_iota(jnp.int32, (16, n), 0)
    stacked = jnp.zeros((16, n), F32)
    for i, piece in enumerate(pieces):
        stacked = jnp.where(at == i, piece, stacked)
    row = lax.broadcasted_iota(jnp.int32, (16, 2 * WIDTH), 0)
    column = lax.broadcasted_iota(jnp.int32, (16, 2 * WIDTH), 1)
    chosen = jnp.where((row >= 3) == (column >= WIDTH), 1.0, 0.0).astype(BF16)
    both = dot(stacked.astype(BF16), chosen, 0, 0)
    return both[:, :WIDTH], both[:, WIDTH:]


def grad_kernel(
    features,
    row_total,
    facts_ref,
    parts_ref,
    attended_ref,
    q_ref,
    gate_ref,
    cotangent_ref,
    gain_ref,
    query_ref,
    own_ref,
    gain_part_ref,
    grad_ref,
    pieces_ref,
    mixed_ref,
    gate_grad_ref,
    query_grad_ref,
):
    total = parts_ref[0]
    for p in range(1, parts_ref.shape[0]):
        total = total + parts_ref[p]
    inverse_row = lax.rsqrt(total[0:1] * (1.0 / features) + EPSILON)
    slope_row = inverse_row * total[1:2] * (1.0 / features)
    decay_on = jnp.exp(-rate_row(facts_ref) * (rows_iota(BLOCK) + 1.0))
    over_block = power(facts_ref, float(BLOCK))
    carried = jnp.zeros((WIDTH, WIDTH), F32)
    gain_sum = jnp.zeros((1, WIDTH), F32)
    blocks = q_ref.shape[0] // BLOCK

    def columns(b):
        lanes = slice(b * BLOCK, (b + 1) * BLOCK)
        return columns_of(inverse_row[:, lanes], slope_row[:, lanes])

    ahead, behind = columns(blocks - 1), None
    for b in reversed(range(-1, blocks)):
        coming = columns(b - 1) if b > 0 else None
        piece = None
        if b >= 0:
            rows = block_rows(b)
            inverse, slope = ahead
            normed = attended_ref[rows] * inverse
            opening = jax.nn.sigmoid(gate_ref[rows].astype(F32))
            grad_open = cotangent_ref[rows].astype(F32) * opening
            gain_sum = gain_sum + jnp.sum(grad_open * normed, axis=0, keepdims=True)
            grad_norm = grad_open * gain_ref[...]
            grad = inverse * (grad_norm - normed * slope)
            piece = dot_split(q_ref[rows], decay_on * grad, 0)
            grad_ref[rows] = beside(*split(grad))
            mixed_ref[rows] = (opening * gain_ref[...] * normed).astype(BF16)
            gate_grad_ref[rows] = (grad_norm * normed * (1.0 - opening)).astype(BF16)
            query_grad_ref[rows] = (
                inverse * (query_ref[0, rows] - inverse * slope * query_ref[1, rows])
            ).astype(BF16)
        if behind is not None:
            pieces_ref[b + 1] = behind
            carried = (carried * over_block + behind) * kept(facts_ref, b + 1)
        ahead, behind = coming, piece
    own_ref[...] = carried
    gain_part_ref[...] = gain_sum * (1.0 / math.sqrt(row_total))


def backward_kernel(
    facts_ref,
    q_ref,
    k_ref,
    v_ref,
    grad_ref,
    mixed_ref,
    gate_grad_ref,
    query_grad_ref,
    mixed_hbm,
    gate_grad_hbm,
    query_grad_hbm,
    key_part_ref,
    value_part_ref,
    sems,
):
    copies = [
        pltpu.make_async_copy(mixed_ref, mixed_hbm.at[0], sems.at[0]),
        pltpu.make_async_copy(gate_grad_ref, gate_grad_hbm.at[0], sems.at[1]),
        pltpu.make_async_copy(query_grad_ref, query_grad_hbm.at[0], sems.at[2]),
    ]
    for copy in copies:
        copy.start()
    weights = decay_matrix(facts_ref, 1)
    blocks = q_ref.shape[0] // BLOCK
    ahead = None
    for b in range(blocks + 1):
        coming = None
        if b < blocks:
            rows = block_rows(b)
            v = v_ref[rows]
            slopes = dot(beside(v, v), grad_ref[rows], 1, 1)
            scores = dot(k_ref[rows], q_ref[rows], 1, 1)
        if ahead is not None:
            (slopes_high, slopes_low), (scores_high, scores_low) = ahead
            before = block_rows(b - 1)
            q, both = q_ref[before], grad_ref[before]
            key_part_ref[before] = dot(slopes_high, q) + dot(slopes_low, q)
            value_part_ref[before] = halves(dot(scores_high, both)) + dot(
                scores_low, both[:, :WIDTH]
            )
        if b < blocks:
            coming = split(slopes * weights), split(scores * weights)
        ahead = coming
    for copy in copies:
        copy.wait()


def finish_kernel(
    tokens,
    place_ref,
    facts_ref,
    all_ref,
    other_ref,
    unbroken_ref,
    pieces_ref,
    k_ref,
    v_ref,
    key_part_ref,
    value_part_ref,
    key_grad_hbm,
    value_grad_hbm,
    gain_grad_hbm,
    gain_row,
    key_rows,
    value_rows,
    sems,
):
    copies = []
    place = place_ref[0]
    chip, core = place // 2, lax.rem(place, 2)
    over_slab = power(facts_ref, float(tokens))
    slabs = all_ref.shape[0]
    state = jnp.zeros((WIDTH, WIDTH), F32)
    along = jnp.ones((1, WIDTH), F32)
    for c in range(slabs // 2):
        after = c > chip
        factor = unbroken_ref[2 * c : 2 * c + 1] * unbroken_ref[2 * c + 1 : 2 * c + 2]
        state = state + chip_state(all_ref, c) * jnp.where(after, along, 0.0)
        along = jnp.where(after, along * (factor * over_slab * over_slab), along)
    partner = unbroken_ref[pl.ds(place - core + 1, 1)]
    state = jnp.where(core == 0, state * (partner * over_slab) + other_ref[...], state)
    gain = all_ref[0, HALF : HALF + 1]
    for s in range(1, slabs):
        gain = gain + all_ref[s, HALF : HALF + 1]
    gain_row[...] = gain
    copies.append(pltpu.make_async_copy(gain_row, gain_grad_hbm, sems.at[2 * (tokens // BLOCK)]))
    copies[0].start()
    decay_back = jnp.exp(-rate_row(facts_ref) * (float(BLOCK - 1) - rows_iota(BLOCK)))
    over_block = power(facts_ref, float(BLOCK))
    last = tokens // BLOCK - 1
    sides = [None] * (last + 1)
    for b in reversed(range(last + 1)):
        if b < last:
            state = state * kept(facts_ref, b + 1)
        sides[b] = split(state)
        state = state * over_block + pieces_ref[b]

    def products(b):
        high, low = sides[b]
        k, v = k_ref[block_rows(b)], v_ref[block_rows(b)]
        return (
            dot(beside(k, k), jnp.concatenate([high, low], axis=0)),
            dot(beside(v, v), beside(high, low), 1, 1),
        )

    ahead = products(last)
    for b in reversed(range(last + 1)):
        coming = products(b - 1) if b > 0 else None
        rows = block_rows(b)
        for i, (product, part, source, target) in enumerate(
            (
                (ahead[0], value_part_ref, value_rows, value_grad_hbm),
                (ahead[1], key_part_ref, key_rows, key_grad_hbm),
            )
        ):
            source[rows] = (part[rows] + decay_back * product).astype(BF16)
            if b % 2 == 0:
                done = pl.ds(b * BLOCK, 2 * BLOCK)
                copy = pltpu.make_async_copy(
                    source.at[done], target.at[0, done], sems.at[2 * b + i]
                )
                copy.start()
                copies.append(copy)
        ahead = coming
    for copy in copies:
        copy.wait()


SMEM = pl.BlockSpec(memory_space=pltpu.SMEM)
VMEM = pl.BlockSpec(memory_space=pltpu.VMEM)
HBM = pl.BlockSpec(memory_space=pltpu.HBM)


def call(kernel, arrays, outs, flops=1 << 24, ins=None, out_specs=None, scratch=()):
    ins = ins or []
    moved = sum(math.prod(a.shape) * a.dtype.itemsize for a in (*arrays, *outs))
    return pl.pallas_call(
        kernel,
        out_shape=outs,
        in_specs=ins + [VMEM] * (len(arrays) - len(ins)),
        out_specs=out_specs or [VMEM] * len(outs),
        scratch_shapes=scratch,
        compiler_params=pltpu.CompilerParams(vmem_limit_bytes=LIMIT),
        cost_estimate=pl.CostEstimate(flops=flops, bytes_accessed=moved, transcendentals=0),
    )(*arrays)


def shape(*dims, dtype=F32):
    return jax.ShapeDtypeStruct(dims, dtype)


def bound(kernel, *fixed):
    def run(*refs):
        kernel(*fixed, *refs)

    return run


def body(queries, key_tokens, values, gate_logits, cotangent, decay_rates, norm_gain, block_starts):
    tokens = queries.shape[1]
    blocks = tokens // BLOCK
    slabs = lax.axis_size("ctx")
    outer, inner = lax.axis_size("dp"), lax.axis_size("pipe")
    features = float(WIDTH * outer * inner)
    place = lax.axis_index("ctx").astype(jnp.int32).reshape(1)
    partners = [(j, j ^ 1) for j in range(slabs)]
    whole = shape(1, tokens, WIDTH, dtype=BF16)
    like = shape(tokens, WIDTH, dtype=BF16)
    wide = shape(tokens, WIDTH)
    states = shape(blocks, WIDTH, WIDTH)
    two_wide = shape(2, tokens, WIDTH)
    dma = pltpu.SemaphoreType.DMA

    gate, cot = (a.reshape(tokens, WIDTH) for a in (gate_logits, cotangent))
    own, pairs, facts, keys, vals, quer, gain = call(
        closing_kernel,
        (
            decay_rates,
            *(
                pltpu.with_memory_space_constraint(a, pltpu.HBM)
                for a in (
                block_starts,
                key_tokens,
                values,
                queries,
                norm_gain,
                )
            ),
        ),
        [
            shape(WIDTH + 8, WIDTH),
            states,
            shape(8, BLOCK),
            like,
            like,
            like,
            shape(1, WIDTH),
        ],
        ins=[SMEM] + [HBM] * 5,
        scratch=[
            pltpu.SMEM((1, blocks), jnp.int32),
            dma((5,)),
        ],
    )
    other = lax.ppermute(own, "ctx", partners)
    (local,) = call(local_kernel, (facts, quer, keys, vals), [wide], flops=1 << 28)
    (half,) = call(
        bound(forward_half_kernel, tokens),
        (place, facts, own, other),
        [shape(HALF + 8, WIDTH)],
        ins=[SMEM],
    )
    everyone = lax.all_gather(half, "ctx")
    attended, states_in, sums, unbroken = call(
        bound(attended_kernel, tokens),
        (place, facts, everyone, other, pairs, quer, local, gate, cot, gain),
        [wide, states, shape(inner, 2, tokens), shape(slabs, WIDTH)],
        ins=[SMEM],
    )
    sums = lax.all_to_all(sums, "pipe", 0, 0, tiled=True)
    (sums,) = call(spread_kernel, (sums,), [shape(outer, 2, tokens)])
    sums = lax.all_to_all(sums, "dp", 0, 0, tiled=True)
    (query_parts,) = call(
        beforehand_kernel,
        (facts, keys, vals, gate, cot, gain, attended, states_in),
        [shape(2, tokens, WIDTH)],
        flops=1 << 30,
    )
    back, gain_part, grad, pieces, mixed, gate_part, query_part = call(
        bound(grad_kernel, features, tokens * slabs),
        (facts, sums, attended, quer, gate, cot, gain, query_parts),
        [
            shape(WIDTH, WIDTH),
            shape(1, WIDTH),
            shape(tokens, 2 * WIDTH, dtype=BF16),
            states,
            like,
            like,
            like,
        ],
    )
    back_other = lax.ppermute(back, "ctx", partners)
    mixed_out, gate_grad, query_grad, key_part, value_part = call(
        backward_kernel,
        (facts, quer, keys, vals, grad, mixed, gate_part, query_part),
        [whole, whole, whole, wide, wide],
        out_specs=[HBM] * 3 + [VMEM] * 2,
        scratch=[dma((3,))],
        flops=1 << 30,
    )
    (back_half,) = call(
        bound(backward_half_kernel, tokens),
        (place, facts, back, back_other, gain_part, unbroken),
        [shape(HALF + 8, WIDTH)],
        ins=[SMEM],
    )
    back_everyone = lax.all_gather(back_half, "ctx")
    key_grad, value_grad, gain_grad = call(
        bound(finish_kernel, tokens),
        (
            place,
            facts,
            back_everyone,
            back_other,
            unbroken,
            pieces,
            keys,
            vals,
            key_part,
            value_part,
        ),
        [whole, whole, shape(1, WIDTH)],
        ins=[SMEM],
        out_specs=[HBM] * 3,
        scratch=[
            pltpu.VMEM((1, WIDTH), F32),
            pltpu.VMEM((tokens, WIDTH), BF16),
            pltpu.VMEM((tokens, WIDTH), BF16),
            dma((2 * blocks + 1,)),
        ],
    )
    return (mixed_out, query_grad, key_grad, value_grad, gate_grad, gain_grad)


def solution(mesh):
    wide = P(None, "ctx", ("dp", "pipe"))
    heads = P(("dp", "pipe"))
    gain = P(("dp", "pipe"), None)
    return jax.shard_map(
        body,
        mesh=mesh,
        in_specs=(wide, wide, wide, wide, wide, heads, gain, P(None, "ctx")),
        out_specs=(wide, wide, wide, wide, wide, gain),
        check_vma=False,
    )
```
